256 devices in a mesh: seq: 16 (over z, core), kvh: 8 (over y_hi, x), batch: 2 (over y_lo).
Axes of the slice: x: 4, y: 4 (y_hi: 2, y_lo: 2; y = y_hi * 2 + y_lo), z: 8, core: 2. Of those that a mesh axis runs over, the one named last changes fastest.
Arguments:
- query: bfloat16 [4096, 5120], P(('batch', 'seq'), 'kvh'), parts along dimension 0, may hold values from -33.3 to 33.3
- self_keys: bfloat16 [4096, 1024], P(('batch', 'seq'), 'kvh'), parts along dimension 0, may hold values from -6.4 to 6.4
- self_values: bfloat16 [4096, 1024], P(('batch', 'seq'), 'kvh'), parts along dimension 0, may hold values from -6 to 6
- cache_keys: bfloat16 [16384, 1024], P(('batch', 'seq'), 'kvh'), parts along dimension 0, may hold values from -6.375 to 6.375
- cache_values: bfloat16 [16384, 1024], P(('batch', 'seq'), 'kvh'), parts along dimension 0, may hold values from -6 to 6
- cache_pos: int32 [16384], P(('batch', 'seq')), parts along dimension 0, may hold values from 0 to 8191, each once
- d_out: bfloat16 [4096, 5120], P(('batch', 'seq'), 'kvh'), parts along dimension 0, may hold values from -6 to 6
Outputs:
- attended: bfloat16 [4096, 5120], P(('batch', 'seq'), 'kvh'), parts along dimension 0
- grad_query: bfloat16 [4096, 5120], P(('batch', 'seq'), 'kvh'), parts along dimension 0
- grad_keys: bfloat16 [4096, 1024], P(('batch', 'seq'), 'kvh'), parts along dimension 0
- grad_values: bfloat16 [4096, 1024], P(('batch', 'seq'), 'kvh'), parts along dimension 0
The draws below stay inside these ranges and needn't reach their ends.
There are 2 independent parts, one for each index of `batch`. The reference program is written for one: setup_inputs(seed, part) draws one part's arguments, and reference() takes and returns one part's arrays. A program takes and returns all parts, laid end to end along the dimension named above; each array names one. Nothing has to cross between parts.
Inputs may be any that keep to these rules, and one draw needn't show every extreme that they name: `cache_pos`: each cache position appears once.
All inputs are finite; a program needn't handle non-finite values.
Results may differ from the reference program's by a relative error of at most 0.012.
The reference program's roundings to bfloat16 on the way count: a program that leaves them out, or rounds other values in their place, can miss the bound.
Values may be sent and summed in bfloat16 or wider, within the bound.
No kernel may reach another device: no remote copies, remote signals or barrier semaphores. Data moves between devices by JAX's collectives and lax.ppermute only.
A program may use at most 64 MiB of HBM per device.

```python
import jax
import jax.numpy as jnp
from jax import lax

HD = 128
GROUP = 5
WINDOW = 512
KV_HEADS = 8
Q_HEADS = 40
TOKENS = 2048
CACHED = 8192


def shared_draw(key):
    base = jax.random.fold_in(key, 907)
    seed_keys, seed_queries = jax.random.split(base, 2)
    key_rows = jnp.clip(jax.random.normal(seed_keys, (TOKENS, KV_HEADS, HD), jnp.float32) * 1.6, -6.375, 6.375)
    query_rows = jnp.clip(jax.random.normal(seed_queries, (TOKENS, KV_HEADS, GROUP, HD), jnp.float32) * 1.6, -6.375, 6.375)
    return (key_rows, query_rows)


def draw_query(key, part):
    key_rows, query_rows = shared_draw(key)
    return query_rows.reshape(TOKENS, KV_HEADS * GROUP * HD).astype(jnp.bfloat16)


def draw_self_keys(key, part):
    key_rows, query_rows = shared_draw(key)
    return key_rows.reshape(TOKENS, KV_HEADS * HD).astype(jnp.bfloat16)


def levels(own_key, dims, cuts, low, largest):
    def one(position, shards_of):
        heights = jax.random.uniform(jax.random.fold_in(jax.random.fold_in(own_key, 6), position), (shards_of,), jnp.float32, low / len(cuts), largest / len(cuts))
        return jnp.repeat(jnp.exp(heights), dims[position] // shards_of).reshape((-1,) + (1,) * (len(dims) - position - 1))

    factor_of = one(*cuts[0])
    for cut in cuts[1:]:
        factor_of = factor_of * one(*cut)
    return factor_of


def centred(stream_key, extent, deviation, reach, cuts=(), kind=jnp.bfloat16):
    drawn = deviation * jax.random.normal(stream_key, extent, jnp.float32)
    if cuts:
        drawn = drawn * levels(stream_key, extent, cuts, -0.22, 0.18)
    return jnp.clip(drawn, -reach, reach).astype(kind)


def setup_inputs(seed: int = 0, part: int = 0) -> dict:
    key_of = jax.random.split(jax.random.key(seed), 8)
    part_splits = jax.random.split(jax.random.fold_in(key_of[7], part), 8)
    return {
        "query": draw_query(jax.random.fold_in(jax.random.fold_in(key_of[7], part), 71), part),
        "self_keys": draw_self_keys(jax.random.fold_in(jax.random.fold_in(key_of[7], part), 71), part),
        "self_values": centred(part_splits[2], (TOKENS, KV_HEADS * HD), 1.0, 6.0, ((0, 16), (1, 8))),
        "cache_keys": centred(part_splits[3], (CACHED, KV_HEADS * HD), 1.6, 6.375, ((0, 16), (1, 8))),
        "cache_values": centred(part_splits[4], (CACHED, KV_HEADS * HD), 1.0, 6.0, ((0, 16), (1, 8))),
        "cache_pos": jax.random.permutation(part_splits[5], CACHED).astype(jnp.int32),
        "d_out": centred(part_splits[6], (TOKENS, Q_HEADS * HD), 1.0, 6.0, ((0, 16), (1, 8))),
    }


row_block = 64


def reference(query, self_keys, self_values, cache_keys, cache_values, cache_pos, d_out):
    scaling = HD ** -0.5
    start_pos = CACHED - TOKENS
    key_all = jnp.concatenate([cache_keys, self_keys], axis=0).astype(jnp.float32).reshape(CACHED + TOKENS, KV_HEADS, HD)
    value_all = jnp.concatenate([cache_values, self_values], axis=0).astype(jnp.float32).reshape(CACHED + TOKENS, KV_HEADS, HD)
    query_all = query.astype(jnp.float32).reshape(TOKENS, KV_HEADS, GROUP, HD)
    grads_all = d_out.astype(jnp.float32).reshape(TOKENS, KV_HEADS, GROUP, HD)
    self_index = jnp.arange(TOKENS, dtype=jnp.int32)

    def one_block(carried, block_no):
        key_acc, value_acc = carried
        first_row = (block_no * row_block).astype(jnp.int32)
        row_index = first_row + jnp.arange(row_block, dtype=jnp.int32)
        queries = lax.dynamic_slice_in_dim(query_all, first_row, row_block, 0)
        grads_out = lax.dynamic_slice_in_dim(grads_all, first_row, row_block, 0)
        bound_pos = start_pos + jnp.maximum(row_index - WINDOW + 1, 0)
        cache_vis = cache_pos[None, :] < bound_pos[:, None]
        self_vis = (self_index[None, :] <= row_index[:, None]) & (self_index[None, :] >= row_index[:, None] - WINDOW + 1)
        visible = jnp.concatenate([cache_vis, self_vis], axis=1)
        scores = jnp.einsum("tkgd,ckd->kgtc", queries, key_all) * scaling
        scores = jnp.where(visible[None, None], scores, -jnp.inf)
        row_max = jnp.max(scores, axis=-1, keepdims=True)
        log_total = row_max + jnp.log(jnp.sum(jnp.exp(scores - row_max), axis=-1, keepdims=True))
        weights = jnp.exp(scores - log_total)
        rounded = lax.optimization_barrier(weights.astype(jnp.bfloat16)).astype(jnp.float32)
        outputs = jnp.einsum("kgtc,ckd->tkgd", rounded, value_all)
        attended = outputs.astype(jnp.bfloat16)
        attended_wide = lax.optimization_barrier(attended).astype(jnp.float32)
        delta_rows = jnp.sum(grads_out * attended_wide, axis=-1)
        grad_weights = jnp.einsum("tkgd,ckd->kgtc", grads_out, value_all)
        grad_scores = weights * (grad_weights - jnp.transpose(delta_rows, (1, 2, 0))[..., None])
        grad_round = lax.optimization_barrier(grad_scores.astype(jnp.bfloat16)).astype(jnp.float32)
        grad_query = (jnp.einsum("kgtc,ckd->tkgd", grad_round, key_all) * scaling).astype(jnp.bfloat16)
        key_acc = key_acc + jnp.einsum("kgtc,tkgd->ckd", grad_round[..., CACHED:], queries)
        value_acc = value_acc + jnp.einsum("kgtc,tkgd->ckd", rounded[..., CACHED:], grads_out)
        return (key_acc, value_acc), (attended.reshape(row_block, Q_HEADS * HD), grad_query.reshape(row_block, Q_HEADS * HD))

    empty = jnp.zeros((TOKENS, KV_HEADS, HD), jnp.float32)
    (key_acc, value_acc), (attended_blocks, query_blocks) = lax.scan(one_block, (empty, empty), jnp.arange(TOKENS // row_block, dtype=jnp.int32))
    attended = attended_blocks.reshape(TOKENS, Q_HEADS * HD)
    grad_query = query_blocks.reshape(TOKENS, Q_HEADS * HD)
    grad_keys = (key_acc * scaling).astype(jnp.bfloat16).reshape(TOKENS, KV_HEADS * HD)
    grad_values = value_acc.astype(jnp.bfloat16).reshape(TOKENS, KV_HEADS * HD)
    return (attended, grad_query, grad_keys, grad_values)
```

```python
import functools

import jax
import jax.numpy as jnp
from jax import lax
from jax.experimental import pallas as pl
from jax.experimental.pallas import tpu as pltpu
from jax.sharding import PartitionSpec as P

HD = 128
GROUP = 5
WINDOW = 512
LANES = 128
NEG = -1e30
SCALE = HD**-0.5
EXP2_SCALE = SCALE * 1.4426950408889634
POS_BASE = 128
POS_ROWS = 16


def nt(a, b):
    return lax.dot_general(a, b, (((1,), (1,)), ((), ())), preferred_element_type=jnp.float32)


def nn(a, b):
    return lax.dot_general(a, b, (((1,), (0,)), ((), ())), preferred_element_type=jnp.float32)


def tn(a, b):
    return lax.dot_general(a, b, (((0,), (0,)), ((), ())), preferred_element_type=jnp.float32)


def group_slices(width):
    return [slice(g * LANES, (g + 1) * LANES) for g in range(width // LANES)]


def attention_kernel(
    meta_ref,
    query_ref,
    grad_ref,
    held_ref,
    pos_ref,
    attended_ref,
    grad_query_ref,
    own_ref,
    back_ref,
    queries,
    grads,
    self_keys,
    self_values,
    weights,
    self_weights,
    row_max,
    row_sum,
    summed,
    delta,
    *,
    rows,
    tile,
    tiles,
    rim,
    start_pos,
):
    total = rows * GROUP
    window = rows * (rim + 1)
    my_index = meta_ref[0]
    base = my_index * rows
    heads = [slice(h * rows, (h + 1) * rows) for h in range(GROUP)]
    cols = [slice(h * HD, (h + 1) * HD) for h in range(GROUP)]
    lanes = group_slices(tile)
    self_lanes = group_slices(window)
    for h in range(GROUP):
        queries[heads[h], :] = query_ref[:, cols[h]]
        grads[heads[h], :] = grad_ref[:, cols[h]]
    for d in range(rim + 1):
        owner = jnp.maximum(my_index - rim + d, 0)
        block = slice(d * rows, (d + 1) * rows)
        self_keys[block, :] = held_ref[owner, tile : tile + rows, :HD]
        self_values[block, :] = held_ref[owner, tile : tile + rows, HD:]

    row = lax.broadcasted_iota(jnp.int32, (rows, LANES), 0)
    lane = lax.broadcasted_iota(jnp.int32, (rows, LANES), 1)
    bound = start_pos + jnp.maximum(base + row - (WINDOW - 1), 0)
    first = window - rows
    self_scores = nt(queries[...], self_keys[...])
    for hs in heads:
        best = None
        for g, ls in enumerate(self_lanes):
            key = lane + g * LANES
            visible = (
                (key <= row + first) & (key >= row + (first - WINDOW + 1)) & (key >= first - base)
            )
            masked = jnp.where(visible, self_scores[hs, ls], NEG)
            self_weights[hs, ls] = masked
            best = masked if best is None else jnp.maximum(best, masked)
        row_max[hs, :] = best

    def score_pass(t, carry):
        scores = nt(queries[...], held_ref[t, :tile, :HD])
        for hs in heads:
            best = row_max[hs, :]
            for ls in lanes:
                masked = jnp.where(pos_ref[t, :, ls] < bound, scores[hs, ls], NEG)
                weights[t, hs, ls] = masked
                best = jnp.maximum(best, masked)
            row_max[hs, :] = best
        return carry

    lax.fori_loop(0, tiles, score_pass, 0)
    row_max[...] = jnp.broadcast_to(
        jnp.max(row_max[...], axis=1, keepdims=True), (total, LANES)
    )

    for hs in heads:
        best = row_max[hs, :]
        added = jnp.zeros((rows, LANES), jnp.float32)
        for ls in self_lanes:
            part = jnp.exp2((self_weights[hs, ls] - best) * EXP2_SCALE)
            self_weights[hs, ls] = part
            added = added + part
        row_sum[hs, :] = added

    def exp_pass(t, carry):
        for hs in heads:
            best = row_max[hs, :]
            added = row_sum[hs, :]
            for ls in lanes:
                part = jnp.exp2((weights[t, hs, ls] - best) * EXP2_SCALE)
                weights[t, hs, ls] = part
                added = added + part
            row_sum[hs, :] = added
        return carry

    lax.fori_loop(0, tiles, exp_pass, 0)
    row_sum[...] = jnp.broadcast_to(
        1.0 / jnp.sum(row_sum[...], axis=1, keepdims=True), (total, LANES)
    )

    def normalised(ref, index, groups):
        parts = []
        for hs in heads:
            inverse = row_sum[hs, :]
            pieces = []
            for ls in groups:
                weight = ref[(*index, hs, ls)] * inverse
                ref[(*index, hs, ls)] = weight
                pieces.append(weight.astype(jnp.bfloat16))
            parts.append(jnp.concatenate(pieces, axis=1))
        return jnp.concatenate(parts, axis=0)

    rounded = normalised(self_weights, (), self_lanes)
    summed[...] = nn(rounded, self_values[...])
    value_grads = tn(rounded, grads[...])
    own_ref[:, HD:] = value_grads[first:, :]
    back_ref[:, HD:] = value_grads[:first, :].astype(jnp.bfloat16)

    def value_pass(t, carry):
        rounded = normalised(weights, (t,), lanes)
        summed[...] += nn(rounded, held_ref[t, :tile, HD:])
        return carry

    lax.fori_loop(0, tiles, value_pass, 0)
    for hs, cs in zip(heads, cols):
        out = summed[hs, :].astype(jnp.bfloat16)
        attended_ref[:, cs] = out
        products = out.astype(jnp.float32) * grads[hs, :].astype(jnp.float32)
        delta[hs, :] = jnp.broadcast_to(jnp.sum(products, axis=1, keepdims=True), (rows, LANES))

    def score_grads(grad_weights, ref, index, groups):
        parts = []
        for hs in heads:
            shift = delta[hs, :]
            pieces = [
                (ref[(*index, hs, ls)] * (grad_weights[hs, ls] - shift)).astype(jnp.bfloat16)
                for ls in groups
            ]
            parts.append(jnp.concatenate(pieces, axis=1))
        return jnp.concatenate(parts, axis=0)

    grad_scores = score_grads(nt(grads[...], self_values[...]), self_weights, (), self_lanes)
    summed[...] = nn(grad_scores, self_keys[...])
    key_grads = tn(grad_scores, queries[...])
    own_ref[:, :HD] = key_grads[first:, :]
    back_ref[:, :HD] = key_grads[:first, :].astype(jnp.bfloat16)

    def grad_pass(t, carry):
        grad_weights = nt(grads[...], held_ref[t, :tile, HD:])
        grad_scores = score_grads(grad_weights, weights, (t,), lanes)
        summed[...] += nn(grad_scores, held_ref[t, :tile, :HD])
        return carry

    lax.fori_loop(0, tiles, grad_pass, 0)
    for hs, cs in zip(heads, cols):
        grad_query_ref[:, cs] = (summed[hs, :] * SCALE).astype(jnp.bfloat16)


def attention(my_index, query, d_out, held, positions, start_pos):
    rows = query.shape[0]
    tiles, tile = positions.shape
    rim = (WINDOW + rows - 2) // rows
    window = rows * (rim + 1)
    total = rows * GROUP
    whole = pl.BlockSpec(memory_space=pltpu.VMEM)
    return pl.pallas_call(
        functools.partial(
            attention_kernel, rows=rows, tile=tile, tiles=tiles, rim=rim, start_pos=start_pos
        ),
        in_specs=[pl.BlockSpec(memory_space=pltpu.SMEM)] + [whole] * 4,
        out_specs=[whole] * 4,
        out_shape=[
            jax.ShapeDtypeStruct((rows, GROUP * HD), jnp.bfloat16),
            jax.ShapeDtypeStruct((rows, GROUP * HD), jnp.bfloat16),
            jax.ShapeDtypeStruct((rows, 2 * HD), jnp.float32),
            jax.ShapeDtypeStruct((window - rows, 2 * HD), jnp.bfloat16),
        ],
        scratch_shapes=[
            pltpu.VMEM((total, HD), jnp.bfloat16),
            pltpu.VMEM((total, HD), jnp.bfloat16),
            pltpu.VMEM((window, HD), jnp.bfloat16),
            pltpu.VMEM((window, HD), jnp.bfloat16),
            pltpu.VMEM((tiles, total, tile), jnp.float32),
            pltpu.VMEM((total, window), jnp.float32),
            pltpu.VMEM((total, LANES), jnp.float32),
            pltpu.VMEM((total, LANES), jnp.float32),
            pltpu.VMEM((total, HD), jnp.float32),
            pltpu.VMEM((total, LANES), jnp.float32),
        ],
        compiler_params=pltpu.CompilerParams(vmem_limit_bytes=58 * 1024 * 1024),
        name="attention",
    )(my_index, query, d_out, held, positions[:, None, :])


def local(query, self_keys, self_values, cache_keys, cache_values, cache_pos, d_out):
    rows = query.shape[0]
    cache_dev = cache_keys.shape[0]
    peers = lax.axis_size("seq")
    my_index = lax.axis_index("seq")
    start_pos = (cache_dev - rows) * peers
    rim = (WINDOW + rows - 2) // rows
    digits = jnp.concatenate([cache_pos // POS_BASE, cache_pos % POS_BASE]).astype(jnp.bfloat16)
    digit_rows = 2 * cache_dev // (2 * HD)
    digits = jnp.pad(digits.reshape(digit_rows, 2 * HD), ((0, POS_ROWS - digit_rows), (0, 0)))
    sent = jnp.concatenate(
        [
            jnp.concatenate([cache_keys, cache_values], axis=1),
            jnp.concatenate([self_keys, self_values], axis=1),
            digits,
        ],
        axis=0,
    )
    held = lax.all_gather(sent, "seq", axis=0)
    got = held[:, cache_dev + rows : cache_dev + rows + digit_rows, :].astype(jnp.int32)
    got = got.reshape(peers, 2, cache_dev)
    positions = got[:, 0] * POS_BASE + got[:, 1]
    attended, grad_query, own, back = attention(
        my_index.reshape(1), query, d_out, held, positions, start_pos
    )
    total = own
    for distance in range(1, rim + 1):
        block = back[(rim - distance) * rows : (rim - distance + 1) * rows]
        route = [(i, i - distance) for i in range(distance, peers)]
        total = total + lax.ppermute(block, "seq", route).astype(jnp.float32)
    grad_keys = (total[:, :HD] * SCALE).astype(jnp.bfloat16)
    grad_values = total[:, HD:].astype(jnp.bfloat16)
    return attended, grad_query, grad_keys, grad_values


def solution(mesh):
    split = P(("batch", "seq"), "kvh")
    return jax.shard_map(
        local,
        mesh=mesh,
        in_specs=(split,) * 5 + (P(("batch", "seq")), split),
        out_specs=(split,) * 4,
        check_vma=False,
    )
```

```python
import functools

import jax
import jax.numpy as jnp
from jax import lax
from jax.experimental import pallas as pl
from jax.experimental.pallas import tpu as pltpu
from jax.sharding import PartitionSpec as P

HD = 128
GROUP = 5
WINDOW = 512
LANES = 128
BLOCK = 32
NEG = -1e30
SCALE = HD**-0.5
EXP2_SCALE = SCALE * 1.4426950408889634
POS_BASE = 128
POS_ROWS = 16


def nt(a, b):
    return lax.dot_general(a, b, (((1,), (1,)), ((), ())), preferred_element_type=jnp.float32)


def nn(a, b):
    return lax.dot_general(a, b, (((1,), (0,)), ((), ())), preferred_element_type=jnp.float32)


def tn(a, b):
    return lax.dot_general(a, b, (((0,), (0,)), ((), ())), preferred_element_type=jnp.float32)


def cuts(width, step):
    return [slice(i, i + step) for i in range(0, width, step)]


def positions_of(digits, groups):
    wide = digits.astype(jnp.float32)
    return wide[:groups] * POS_BASE + wide[groups : 2 * groups]


def row_bound(base, rows, start_pos):
    row = lax.broadcasted_iota(jnp.int32, (rows, LANES), 0)
    bound = start_pos + jnp.maximum(base + row - (WINDOW - 1), 0)
    return bound.astype(jnp.float32)


def window_visible(base, rows, window, g):
    row = lax.broadcasted_iota(jnp.int32, (rows, LANES), 0)
    key = lax.broadcasted_iota(jnp.int32, (rows, LANES), 1) + g * LANES
    first = window - rows
    return (key <= row + first) & (key >= row + (first - WINDOW + 1)) & (key >= first - base)


def accumulate(parts, row_max, row_sum, rs):
    old = row_max[rs, :]
    best = old
    for part in parts:
        best = jnp.maximum(best, part)
    added = row_sum[rs, :] * jnp.exp2((old - best) * EXP2_SCALE)
    for part in parts:
        added = added + jnp.exp2((part - best) * EXP2_SCALE)
    row_max[rs, :] = best
    row_sum[rs, :] = added


def packet_stats(queries, keys, digits, bound, row_max, row_sum, rows):
    tile = keys.shape[0]
    lanes = cuts(tile, LANES)
    positions = positions_of(digits, len(lanes))
    scores = nt(queries, keys)
    for rs in cuts(rows * GROUP, BLOCK):
        inner = slice(rs.start % rows, rs.start % rows + BLOCK)
        limit = bound[inner]
        parts = [
            jnp.where(positions[g : g + 1] < limit, scores[rs, ls], NEG)
            for g, ls in enumerate(lanes)
        ]
        accumulate(parts, row_max, row_sum, rs)


def stats_kernel(*refs, rows, tile, start_pos, packets, fresh, with_window):
    refs = list(refs)
    meta_ref, queries_ref = refs[:2]
    refs = refs[2:]
    if not fresh:
        max_in, sum_in = refs[:2]
        refs = refs[2:]
    packet_refs = refs[:packets]
    refs = refs[packets:]
    if with_window:
        window_ref = refs[0]
        refs = refs[1:]
    row_max, row_sum = refs
    base = meta_ref[0] * rows
    bound = row_bound(base, rows, start_pos)
    if fresh:
        row_max[...] = jnp.full(row_max.shape, NEG, jnp.float32)
        row_sum[...] = jnp.zeros(row_sum.shape, jnp.float32)
    else:
        row_max[...] = max_in[...]
        row_sum[...] = sum_in[...]
    for packet in packet_refs:
        for n in range(packet.shape[0]):
            packet_stats(
                queries_ref[...],
                packet[n, :tile, :],
                packet[n, tile : tile + POS_ROWS, :],
                bound,
                row_max,
                row_sum,
                rows,
            )
    if with_window:
        window = window_ref.shape[0]
        scores = nt(queries_ref[...], window_ref[:, :HD])
        lanes = cuts(window, LANES)
        shown = [window_visible(base, rows, window, g) for g in range(len(lanes))]
        for rs in cuts(rows * GROUP, BLOCK):
            inner = slice(rs.start % rows, rs.start % rows + BLOCK)
            parts = [
                jnp.where(shown[g][inner], scores[rs, ls], NEG) for g, ls in enumerate(lanes)
            ]
            accumulate(parts, row_max, row_sum, rs)


def stats(my_index, queries, previous, packets, window, rows, tile, start_pos):
    total = rows * GROUP
    whole = pl.BlockSpec(memory_space=pltpu.VMEM)
    state = jax.ShapeDtypeStruct((total, LANES), jnp.float32)
    fresh = previous is None
    operands = [queries] + ([] if fresh else list(previous)) + list(packets)
    if window is not None:
        operands.append(window)
    keys = sum(p.shape[0] for p in packets) * tile
    return pl.pallas_call(
        functools.partial(
            stats_kernel,
            rows=rows,
            tile=tile,
            start_pos=start_pos,
            packets=len(packets),
            fresh=fresh,
            with_window=window is not None,
        ),
        in_specs=[pl.BlockSpec(memory_space=pltpu.SMEM)] + [whole] * len(operands),
        out_specs=[whole] * 2,
        out_shape=[state, state],
        cost_estimate=pl.CostEstimate(
            flops=2 * total * HD * keys, transcendentals=total * keys, bytes_accessed=2 * keys * HD
        ),
        name="stats",
    )(my_index, *operands)


def final_kernel(*refs, rows, tile, start_pos, counts, last):
    refs = list(refs)
    meta_ref, queries, grads, window_ref, max_in, sum_in = refs[:6]
    refs = refs[6:]
    key_packets = refs[: len(counts)]
    value_packets = refs[len(counts) : 2 * len(counts)]
    refs = refs[2 * len(counts) :]
    attended_ref, grad_query_ref, own_ref, back_ref = refs[:4]
    (keys, values, weights, self_weights, row_max, row_sum, summed, delta, key_sems, value_sems) = (
        refs[4:]
    )
    total = rows * GROUP
    window = window_ref.shape[0]
    tiles = sum(counts)
    base = meta_ref[0] * rows
    heads = cuts(total, rows)
    cols = cuts(GROUP * HD, HD)
    lanes = cuts(tile, LANES)
    self_lanes = cuts(window, LANES)
    first = window - rows

    copies = []
    at = 0
    for n, count in enumerate(counts):
        rows_kept = tile + POS_ROWS
        copies.append(
            (
                pltpu.make_async_copy(
                    key_packets[n].at[:, pl.ds(0, rows_kept), :],
                    keys.at[pl.ds(at, count)],
                    key_sems.at[n],
                ),
                pltpu.make_async_copy(
                    value_packets[n].at[:, pl.ds(0, tile), :],
                    values.at[pl.ds(at, count)],
                    value_sems.at[n],
                ),
            )
        )
        at += count
    for n in reversed(range(len(counts))):
        copies[n][0].start()
    for n in range(len(counts)):
        copies[n][1].start()

    bound = row_bound(base, rows, start_pos)
    row_max[...] = max_in[...]
    row_sum[...] = sum_in[...]
    for n in reversed(range(len(counts))):
        copies[n][0].wait()
    for t in range(tiles - last, tiles):
        packet_stats(
            queries[...],
            keys[t, :tile, :],
            keys[t, tile:, :],
            bound,
            row_max,
            row_sum,
            rows,
        )
    for hs in heads:
        best = row_max[hs, :]
        top = jnp.max(best, axis=1, keepdims=True)
        scaled = row_sum[hs, :] * jnp.exp2((best - top) * EXP2_SCALE)
        log_total = top + jnp.log(jnp.sum(scaled, axis=1, keepdims=True)) * (1.0 / SCALE)
        row_max[hs, :] = jnp.broadcast_to(log_total, (rows, LANES))

    self_scores = nt(queries[...], window_ref[:, :HD])
    shown = [window_visible(base, rows, window, g) for g in range(len(self_lanes))]
    parts = []
    for hs in heads:
        log_total = row_max[hs, :]
        pieces = []
        for g, ls in enumerate(self_lanes):
            weight = jnp.exp2((self_scores[hs, ls] - log_total) * EXP2_SCALE)
            weight = jnp.where(shown[g], weight, 0.0)
            self_weights[hs, ls] = weight
            pieces.append(weight.astype(jnp.bfloat16))
        parts.append(jnp.concatenate(pieces, axis=1))
    rounded = jnp.concatenate(parts, axis=0)
    summed[...] = nn(rounded, window_ref[:, HD:])
    value_grads = tn(rounded, grads[...])
    own_ref[:, HD:] = value_grads[first:, :]
    back_ref[:, HD:] = value_grads[:first, :].astype(jnp.bfloat16)
    for n in range(len(counts)):
        copies[n][1].wait()

    def value_pass(t, carry):
        positions = positions_of(keys[t, tile:, :], len(lanes))
        scores = nt(queries[...], keys[t, :tile, :])
        parts = []
        for hs in heads:
            log_total = row_max[hs, :]
            pieces = []
            for g, ls in enumerate(lanes):
                weight = jnp.exp2((scores[hs, ls] - log_total) * EXP2_SCALE)
                weight = jnp.where(positions[g : g + 1] < bound, weight, 0.0)
                weights[t, hs, ls] = weight
                pieces.append(weight.astype(jnp.bfloat16))
            parts.append(jnp.concatenate(pieces, axis=1))
        summed[...] += nn(jnp.concatenate(parts, axis=0), values[t])
        return carry

    lax.fori_loop(0, tiles, value_pass, 0)
    for hs, cs in zip(heads, cols):
        out = summed[hs, :].astype(jnp.bfloat16)
        attended_ref[:, cs] = out
        products = out.astype(jnp.float32) * grads[hs, :].astype(jnp.float32)
        delta[hs, :] = jnp.broadcast_to(jnp.sum(products, axis=1, keepdims=True), (rows, LANES))

    def score_grads(grad_weights, ref, index, groups):
        parts = []
        for hs in heads:
            shift = delta[hs, :]
            pieces = [
                (ref[(*index, hs, ls)] * (grad_weights[hs, ls] - shift)).astype(jnp.bfloat16)
                for ls in groups
            ]
            parts.append(jnp.concatenate(pieces, axis=1))
        return jnp.concatenate(parts, axis=0)

    grad_scores = score_grads(nt(grads[...], window_ref[:, HD:]), self_weights, (), self_lanes)
    summed[...] = nn(grad_scores, window_ref[:, :HD])
    key_grads = tn(grad_scores, queries[...])
    own_ref[:, :HD] = key_grads[first:, :]
    back_ref[:, :HD] = key_grads[:first, :].astype(jnp.bfloat16)

    def grad_pass(t, carry):
        grad_weights = nt(grads[...], values[t])
        grad_scores = score_grads(grad_weights, weights, (t,), lanes)
        summed[...] += nn(grad_scores, keys[t, :tile, :])
        return carry

    lax.fori_loop(0, tiles, grad_pass, 0)
    for hs, cs in zip(heads, cols):
        grad_query_ref[:, cs] = (summed[hs, :] * SCALE).astype(jnp.bfloat16)


def final(my_index, queries, grads, window, state, key_packets, value_packets, rows, tile, start_pos):
    counts = tuple(p.shape[0] for p in key_packets)
    tiles = sum(counts)
    total = rows * GROUP
    span = window.shape[0]
    whole = pl.BlockSpec(memory_space=pltpu.VMEM)
    anywhere = pl.BlockSpec(memory_space=pl.ANY)
    f32, bf16 = jnp.float32, jnp.bfloat16
    return pl.pallas_call(
        functools.partial(
            final_kernel, rows=rows, tile=tile, start_pos=start_pos, counts=counts, last=2
        ),
        in_specs=[pl.BlockSpec(memory_space=pltpu.SMEM)]
        + [whole] * 5
        + [anywhere] * (2 * len(counts)),
        out_specs=[whole] * 4,
        out_shape=[
            jax.ShapeDtypeStruct((rows, GROUP * HD), bf16),
            jax.ShapeDtypeStruct((rows, GROUP * HD), bf16),
            jax.ShapeDtypeStruct((rows, 2 * HD), f32),
            jax.ShapeDtypeStruct((span - rows, 2 * HD), bf16),
        ],
        scratch_shapes=[
            pltpu.VMEM((tiles, tile + POS_ROWS, HD), bf16),
            pltpu.VMEM((tiles, tile, HD), bf16),
            pltpu.VMEM((tiles, total, tile), f32),
            pltpu.VMEM((total, span), f32),
            pltpu.VMEM((total, LANES), f32),
            pltpu.VMEM((total, LANES), f32),
            pltpu.VMEM((total, HD), f32),
            pltpu.VMEM((total, LANES), f32),
            pltpu.SemaphoreType.DMA((len(counts),)),
            pltpu.SemaphoreType.DMA((len(counts),)),
        ],
        compiler_params=pltpu.CompilerParams(vmem_limit_bytes=56 * 1024 * 1024),
        cost_estimate=pl.CostEstimate(
            flops=8 * total * HD * tiles * tile,
            transcendentals=total * tiles * tile,
            bytes_accessed=4 * tiles * tile * HD,
        ),
        name="final",
    )(my_index, queries, grads, window, *state, *key_packets, *value_packets)


def local(query, self_keys, self_values, cache_keys, cache_values, cache_pos, d_out):
    rows = query.shape[0]
    tile = cache_keys.shape[0]
    peers = lax.axis_size("seq")
    my_index = lax.axis_index("seq")
    start_pos = (tile - rows) * peers
    rim = (WINDOW + rows - 2) // rows
    chips = peers // 2
    kept = tile + POS_ROWS
    even = my_index % 2 == 0

    partner = [(i, i ^ 1) for i in range(peers)]
    ring = [(2 * z, 2 * ((z + 1) % chips)) for z in range(chips)]
    ring += [(2 * z + 1, 2 * ((z - 1) % chips) + 1) for z in range(chips)]

    def swap(block):
        return lax.ppermute(block, "seq", partner)

    def turn(block):
        return lax.ppermute(block, "seq", ring)

    digits = jnp.concatenate([cache_pos // POS_BASE, cache_pos % POS_BASE]).astype(jnp.bfloat16)
    digits = digits.reshape(2 * tile // HD, HD)
    digits = jnp.pad(digits, ((0, POS_ROWS - digits.shape[0]), (0, 0)))
    own_keys = jnp.concatenate([cache_keys, digits, self_keys])[None]
    own_values = jnp.concatenate([cache_values, self_values])[None]
    key_pair = jnp.concatenate([own_keys, swap(own_keys)])
    value_pair = jnp.concatenate([own_values, swap(own_values)])
    key_steps, value_steps = [], []
    key_block, value_block = key_pair, value_pair
    for step in range(1, chips // 2 + 1):
        if step == 3:
            key_block, value_block = key_block[:, :kept], value_block[:, :tile]
        if step == chips // 2:
            key_block, value_block = key_block[:1], value_block[:1]
        key_block, value_block = turn(key_block), turn(value_block)
        key_steps.append((key_block, swap(key_block)))
        value_steps.append((value_block, swap(value_block)))

    def stacked(heads):
        heads = heads.reshape(rows, GROUP, HD)
        return jnp.transpose(heads, (1, 0, 2)).reshape(GROUP * rows, HD)

    queries, grads = stacked(query), stacked(d_out)

    def tails(pair, start):
        return jnp.where(even, pair[0][:, start:], pair[1][:, start:])

    def window_of(own, one, two):
        if_even = jnp.concatenate([two[0], two[1], one[0], one[1], own[0]])
        if_odd = jnp.concatenate([two[1], one[0], one[1], own[1], own[0]])
        return jnp.where(even, if_even, if_odd)

    window = jnp.concatenate(
        [
            window_of(key_pair[:, kept:], tails(key_steps[0], kept), tails(key_steps[1], kept)),
            window_of(value_pair[:, tile:], tails(value_steps[0], tile), tails(value_steps[1], tile)),
        ],
        axis=1,
    )
    index = my_index.reshape(1)
    shape = (rows, tile, start_pos)
    state = stats(index, queries, None, [key_pair], None, *shape)
    state = stats(index, queries, state, key_steps[0], None, *shape)
    state = stats(index, queries, state, key_steps[1], window, *shape)
    state = stats(index, queries, state, key_steps[2], None, *shape)
    key_packets = [key_pair] + [block for step in key_steps for block in step]
    value_packets = [value_pair] + [block for step in value_steps for block in step]
    attended, grad_query, own, back = final(
        index, queries, grads, window, state, key_packets, value_packets, *shape
    )
    total = own
    for distance in range(1, rim + 1):
        block = back[(rim - distance) * rows : (rim - distance + 1) * rows]
        route = [(i, i - distance) for i in range(distance, peers)]
        total = total + lax.ppermute(block, "seq", route).astype(jnp.float32)
    grad_keys = (total[:, :HD] * SCALE).astype(jnp.bfloat16)
    grad_values = total[:, HD:].astype(jnp.bfloat16)
    return attended, grad_query, grad_keys, grad_values


def solution(mesh):
    split = P(("batch", "seq"), "kvh")
    return jax.shard_map(
        local,
        mesh=mesh,
        in_specs=(split,) * 5 + (P(("batch", "seq")), split),
        out_specs=(split,) * 4,
        check_vma=False,
    )
```

```python
import functools

import jax
import jax.numpy as jnp
from jax import lax
from jax.experimental import pallas as pl
from jax.experimental.pallas import tpu as pltpu
from jax.sharding import PartitionSpec as P


HD = 128
GROUP = 5
WINDOW = 512
LANES = 128
BLOCK = 32
NEG = -1e30
SCALE = HD**-0.5
EXP2_SCALE = SCALE * 1.4426950408889634
POS_BASE = 128
POS_ROWS = 16


def nt(a, b):
    return lax.dot_general(a, b, (((1,), (1,)), ((), ())), preferred_element_type=jnp.float32)


def nn(a, b):
    return lax.dot_general(a, b, (((1,), (0,)), ((), ())), preferred_element_type=jnp.float32)


def tn(a, b):
    return lax.dot_general(a, b, (((0,), (0,)), ((), ())), preferred_element_type=jnp.float32)


def cuts(width, step):
    return [slice(i, i + step) for i in range(0, width, step)]


def positions_of(digits, groups):
    wide = digits.astype(jnp.float32)
    return wide[:groups] * POS_BASE + wide[groups : 2 * groups]


def row_bound(base, rows, start_pos):
    row = lax.broadcasted_iota(jnp.int32, (rows, LANES), 0)
    bound = start_pos + jnp.maximum(base + row - (WINDOW - 1), 0)
    return bound.astype(jnp.float32)


def window_visible(base, rows, window, g):
    row = lax.broadcasted_iota(jnp.int32, (rows, LANES), 0)
    key = lax.broadcasted_iota(jnp.int32, (rows, LANES), 1) + g * LANES
    first = window - rows
    return (key <= row + first) & (key >= row + (first - WINDOW + 1)) & (key >= first - base)


def accumulate(parts, row_max, row_sum, rs):
    old = row_max[rs, :]
    best = old
    for part in parts:
        best = jnp.maximum(best, part)
    added = row_sum[rs, :] * jnp.exp2((old - best) * EXP2_SCALE)
    raised = [jnp.exp2((part - best) * EXP2_SCALE) for part in parts]
    for part in raised:
        added = added + part
    row_max[rs, :] = best
    row_sum[rs, :] = added
    return raised, best


def packet_stats(queries, keys, digits, bound, state, rows, t):
    row_max, row_sum, raised_ref, level_ref = state
    lanes = cuts(keys.shape[0], LANES)
    positions = positions_of(digits, len(lanes))
    scores = nt(queries, keys)
    for rs in cuts(rows * GROUP, BLOCK):
        inner = slice(rs.start % rows, rs.start % rows + BLOCK)
        limit = bound[inner]
        parts = [
            jnp.where(positions[g : g + 1] < limit, scores[rs, ls], NEG)
            for g, ls in enumerate(lanes)
        ]
        raised, best = accumulate(parts, row_max, row_sum, rs)
        for ls, part in zip(lanes, raised):
            raised_ref[t, rs, ls] = part
        level_ref[t, rs, :] = best


def stats_kernel(*refs, rows, tile, start_pos, counts, done, with_window):
    meta_ref = refs[0]
    first_packet = 2 if done else 3
    packets = refs[first_packet : first_packet + len(counts)]
    at = first_packet + len(counts) + (5 if with_window else 0) + (4 if done else 0)
    outs = refs[at:]
    state = outs[:4]
    if done:
        queries_ref = refs[1]
    else:
        queries_ref, grads_ref = outs[4:]
        for h in range(GROUP):
            queries_ref[h * rows : (h + 1) * rows, :] = refs[1][:, h * HD : (h + 1) * HD]
            grads_ref[h * rows : (h + 1) * rows, :] = refs[2][:, h * HD : (h + 1) * HD]
    row_max, row_sum = state[:2]
    base = meta_ref[0] * rows
    bound = row_bound(base, rows, start_pos)
    if done:
        max_in, sum_in = refs[at - 4 : at - 2]
        row_max[...] = max_in[...]
        row_sum[...] = sum_in[...]
    else:
        row_max[...] = jnp.full(row_max.shape, NEG, jnp.float32)
        row_sum[...] = jnp.zeros(row_sum.shape, jnp.float32)
    t = done
    for packet, count in zip(packets, counts):

        def one(n, carry, packet=packet, t=t):
            packet_stats(
                queries_ref[...],
                packet[n, :tile, :],
                packet[n, tile : tile + POS_ROWS, :],
                bound,
                state,
                rows,
                t + n,
            )
            return carry

        lax.fori_loop(0, count, one, 0)
        t += count
    if with_window:
        self_raised, self_level, window_ref = outs[4:]
        own, up_one, swapped_one, up_two, swapped_two = refs[first_packet + len(counts) :][:5]
        even = meta_ref[0] % 2 == 0

        def place(blocks):
            for d, block in enumerate(blocks):
                window_ref[d * rows : (d + 1) * rows, :] = block

        @pl.when(even)
        def _():
            place([up_two[0], up_two[1], up_one[0], up_one[1], own[0]])

        @pl.when(jnp.logical_not(even))
        def _():
            place([swapped_two[1], swapped_one[0], swapped_one[1], own[1], own[0]])

        window = window_ref.shape[0]
        scores = nt(queries_ref[...], window_ref[:, :HD])
        lanes = cuts(window, LANES)
        shown = [window_visible(base, rows, window, g) for g in range(len(lanes))]
        for rs in cuts(rows * GROUP, BLOCK):
            inner = slice(rs.start % rows, rs.start % rows + BLOCK)
            parts = [
                jnp.where(shown[g][inner], scores[rs, ls], NEG) for g, ls in enumerate(lanes)
            ]
            raised, best = accumulate(parts, row_max, row_sum, rs)
            for ls, part in zip(lanes, raised):
                self_raised[rs, ls] = part
            self_level[rs, :] = best


WHOLE = pl.BlockSpec(memory_space=pltpu.VMEM)
ANYWHERE = pl.BlockSpec(memory_space=pl.ANY)
SCALARS = pl.BlockSpec(memory_space=pltpu.SMEM)
LIMIT = pltpu.CompilerParams(vmem_limit_bytes=6 * 1024 * 1024)


def f32(*shape):
    return jax.ShapeDtypeStruct(shape, jnp.float32)


def bf16(*shape):
    return jax.ShapeDtypeStruct(shape, jnp.bfloat16)


def stats(my_index, inputs, previous, packets, selfs, done, tiles, rows, tile, start_pos):
    total = rows * GROUP
    counts = tuple(p.shape[0] for p in packets)
    operands = [my_index, *inputs, *packets]
    outs = [f32(total, LANES), f32(total, LANES), f32(tiles, total, tile), f32(tiles, total, LANES)]
    aliases = {}
    if selfs is not None:
        operands += list(selfs)
        span = (WINDOW // rows + 1) * rows
        outs += [f32(total, span), f32(total, LANES), bf16(span, 2 * HD)]
    if previous is None:
        outs += [bf16(total, HD)] * 2
    else:
        aliases = {len(operands) + 2: 2, len(operands) + 3: 3}
        operands += list(previous)
    keys = sum(counts) * tile
    return pl.pallas_call(
        functools.partial(
            stats_kernel,
            rows=rows,
            tile=tile,
            start_pos=start_pos,
            counts=counts,
            done=done,
            with_window=selfs is not None,
        ),
        in_specs=[SCALARS] + [WHOLE] * (len(operands) - 1),
        out_specs=[WHOLE] * len(outs),
        out_shape=outs,
        input_output_aliases=aliases,
        compiler_params=LIMIT,
        cost_estimate=pl.CostEstimate(
            flops=2 * total * HD * keys, transcendentals=total * keys, bytes_accessed=2 * keys * HD
        ),
        name="stats",
    )(*operands)


def fetch_all(packets, counts, held, sems, width):
    copies = []
    at = 0
    for n, count in enumerate(counts):
        copy = pltpu.make_async_copy(
            packets[n].at[:, pl.ds(0, width), :], held.at[pl.ds(at, count)], sems.at[n]
        )
        copy.start()
        copies.append(copy)
        at += count
    return copies


def value_kernel(*refs, rows, tile, counts):
    n = len(counts)
    (queries, grads, window_ref, max_in, sum_in, raised, level, self_raised, self_level) = refs[:9]
    key_packets = refs[9 : 9 + n]
    value_packets = refs[9 + n : 9 + 2 * n]
    outs = refs[9 + 2 * n :]
    (attended_ref, factor_ref, delta, partial_ref, keys, values, own_ref) = outs[:7]
    rim = window_ref.shape[0] // rows - 1
    back_refs = outs[7 : 7 + rim]
    (top_ref, inverse_ref, summed, self_weights, key_sems, value_sems) = outs[7 + rim :]
    copies = fetch_all(value_packets, counts, values, value_sems, tile)
    key_copies = fetch_all(key_packets, counts, keys, key_sems, tile)
    total = rows * GROUP
    window = window_ref.shape[0]
    tiles = sum(counts)
    heads = cuts(total, rows)
    cols = cuts(GROUP * HD, HD)
    lanes = cuts(tile, LANES)
    self_lanes = cuts(window, LANES)
    first = window - rows
    for hs in heads:
        best = max_in[hs, :]
        top = jnp.max(best, axis=1, keepdims=True)
        scaled = sum_in[hs, :] * jnp.exp2((best - top) * EXP2_SCALE)
        top_ref[hs, :] = jnp.broadcast_to(top, (rows, LANES))
        inverse = 1.0 / jnp.sum(scaled, axis=1, keepdims=True)
        inverse_ref[hs, :] = jnp.broadcast_to(inverse, (rows, LANES))

    parts = []
    for hs in heads:
        factor = jnp.exp2((self_level[hs, :] - top_ref[hs, :]) * EXP2_SCALE) * inverse_ref[hs, :]
        pieces = []
        for ls in self_lanes:
            weight = self_raised[hs, ls] * factor
            self_weights[hs, ls] = weight
            pieces.append(weight.astype(jnp.bfloat16))
        parts.append(jnp.concatenate(pieces, axis=1))
    rounded = jnp.concatenate(parts, axis=0)
    summed[...] = nn(rounded, window_ref[:, HD:])
    value_grads = tn(rounded, grads[...])
    own_ref[:, HD:] = value_grads[first:, :]
    for d, back_ref in enumerate(back_refs):
        back_ref[:, HD:] = value_grads[d * rows : (d + 1) * rows, :].astype(jnp.bfloat16)
    for copy in copies:
        copy.wait()

    def value_pass(t, carry):
        parts = []
        for hs in heads:
            factor = jnp.exp2((level[t, hs, :] - top_ref[hs, :]) * EXP2_SCALE) * inverse_ref[hs, :]
            factor_ref[t, hs, :] = factor
            pieces = [(raised[t, hs, ls] * factor).astype(jnp.bfloat16) for ls in lanes]
            parts.append(jnp.concatenate(pieces, axis=1))
        summed[...] += nn(jnp.concatenate(parts, axis=0), values[t])
        return carry

    lax.fori_loop(0, tiles, value_pass, 0)
    for hs, cs in zip(heads, cols):
        out = summed[hs, :].astype(jnp.bfloat16)
        attended_ref[:, cs] = out
        products = out.astype(jnp.float32) * grads[hs, :].astype(jnp.float32)
        delta[hs, :] = jnp.broadcast_to(jnp.sum(products, axis=1, keepdims=True), (rows, LANES))

    grad_weights = nt(grads[...], window_ref[:, HD:])
    parts = []
    for hs in heads:
        shift = delta[hs, :]
        pieces = [
            (self_weights[hs, ls] * (grad_weights[hs, ls] - shift)).astype(jnp.bfloat16)
            for ls in self_lanes
        ]
        parts.append(jnp.concatenate(pieces, axis=1))
    grad_scores = jnp.concatenate(parts, axis=0)
    partial_ref[...] = nn(grad_scores, window_ref[:, :HD])
    key_grads = tn(grad_scores, queries[...])
    own_ref[:, :HD] = key_grads[first:, :]
    for d, back_ref in enumerate(back_refs):
        back_ref[:, :HD] = key_grads[d * rows : (d + 1) * rows, :].astype(jnp.bfloat16)
    for copy in key_copies:
        copy.wait()


def grad_kernel(
    grads, raised, factor_ref, delta, partial_ref, keys, values, out_ref, *scratch, rows, span, last
):
    heads = cuts(rows * GROUP, rows)
    cols = cuts(GROUP * HD, HD)
    lanes = cuts(keys.shape[1], LANES)
    summed = scratch[0] if last else out_ref
    summed[...] = partial_ref[...]

    def grad_pass(t, carry):
        grad_weights = nt(grads[...], values[t])
        parts = []
        for hs in heads:
            shift = delta[hs, :]
            factor = factor_ref[t, hs, :]
            pieces = [
                (raised[t, hs, ls] * factor * (grad_weights[hs, ls] - shift)).astype(jnp.bfloat16)
                for ls in lanes
            ]
            parts.append(jnp.concatenate(pieces, axis=1))
        summed[...] += nn(jnp.concatenate(parts, axis=0), keys[t])
        return carry

    lax.fori_loop(*span, grad_pass, 0)
    if last:
        for hs, cs in zip(heads, cols):
            out_ref[:, cs] = (summed[hs, :] * SCALE).astype(jnp.bfloat16)


def combine_kernel(own_ref, *refs):
    total = own_ref[...]
    for ref in refs[:-2]:
        total = total + ref[...].astype(jnp.float32)
    refs[-2][...] = (total[:, :HD] * SCALE).astype(jnp.bfloat16)
    refs[-1][...] = total[:, HD:].astype(jnp.bfloat16)


def value_stage(queries, grads, window, state, key_packets, value_packets, rows, tile):
    counts = tuple(p.shape[0] for p in value_packets)
    tiles = sum(counts)
    total = rows * GROUP
    span = window.shape[0]
    rim = span // rows - 1
    return pl.pallas_call(
        functools.partial(value_kernel, rows=rows, tile=tile, counts=counts),
        in_specs=[WHOLE] * 9 + [ANYWHERE] * (2 * len(counts)),
        out_specs=[WHOLE] * (7 + rim),
        out_shape=[
            bf16(rows, GROUP * HD),
            f32(tiles, total, LANES),
            f32(total, LANES),
            f32(total, HD),
            bf16(tiles, tile, HD),
            bf16(tiles, tile, HD),
            f32(rows, 2 * HD),
        ]
        + [bf16(rows, 2 * HD)] * rim,
        scratch_shapes=[
            pltpu.VMEM((total, LANES), jnp.float32),
            pltpu.VMEM((total, LANES), jnp.float32),
            pltpu.VMEM((total, HD), jnp.float32),
            pltpu.VMEM((total, span), jnp.float32),
            pltpu.SemaphoreType.DMA((len(counts),)),
            pltpu.SemaphoreType.DMA((len(counts),)),
        ],
        input_output_aliases={6: 1},
        compiler_params=LIMIT,
        cost_estimate=pl.CostEstimate(
            flops=2 * total * HD * tiles * tile, transcendentals=0, bytes_accessed=tiles * tile * HD
        ),
        name="value_stage",
    )(queries, grads, window, *state, *key_packets, *value_packets)


def grad_stage(grads, raised, factor, delta, partial, keys, values, rows, span, last):
    tiles, tile, _ = keys.shape
    total = rows * GROUP
    return pl.pallas_call(
        functools.partial(grad_kernel, rows=rows, span=span, last=last),
        in_specs=[WHOLE] * 7,
        out_specs=WHOLE,
        out_shape=bf16(rows, GROUP * HD) if last else f32(total, HD),
        scratch_shapes=[pltpu.VMEM((total, HD), jnp.float32)] if last else [],
        compiler_params=LIMIT,
        cost_estimate=pl.CostEstimate(
            flops=4 * total * HD * (span[1] - span[0]) * tile,
            transcendentals=0,
            bytes_accessed=tiles * tile * HD,
        ),
        name="grad_stage",
    )(grads, raised, factor, delta, partial, keys, values)


def combine(own, returned):
    rows = own.shape[0]
    return pl.pallas_call(
        combine_kernel,
        in_specs=[WHOLE] * (1 + len(returned)),
        out_specs=[WHOLE] * 2,
        out_shape=[bf16(rows, HD)] * 2,
        compiler_params=LIMIT,
        name="combine",
    )(own, *returned)


def compute(index, query, d_out, key_groups, value_groups, selfs, selfs_at, shape):
    rows, tile, start_pos = shape
    tiles = sum(p.shape[0] for group in key_groups for p in group)
    state, done = None, 0
    for n, group in enumerate(key_groups):
        inputs = [queries] if done else [query, d_out]
        extra = selfs if n == selfs_at else None
        outs = stats(index, inputs, state, group, extra, done, tiles, rows, tile, start_pos)
        state = outs[:4]
        if not done:
            queries, grads = outs[4:]
        elif extra is not None:
            *self_state, window = outs[4:]
        done += sum(p.shape[0] for p in group)
    key_packets = [p for group in key_groups for p in group]
    value_packets = [p for group in value_groups for p in group]
    attended, factor, delta, partial, keys, values, own, *back = value_stage(
        queries, grads, window, [*state, *self_state], key_packets, value_packets, rows, tile
    )

    def finish():
        shared = (grads, state[2], factor, delta)
        summed = grad_stage(*shared, partial, keys, values, rows, (0, tiles // 2), False)
        return grad_stage(*shared, summed, keys, values, rows, (tiles // 2, tiles), True)

    return attended, finish, own, back


def local(query, self_keys, self_values, cache_keys, cache_values, cache_pos, d_out):
    rows = query.shape[0]
    tile = cache_keys.shape[0]
    peers = lax.axis_size("seq")
    my_index = lax.axis_index("seq")
    start_pos = (tile - rows) * peers
    rim = (WINDOW + rows - 2) // rows
    chips = peers // 2

    partner = [(i, i ^ 1) for i in range(peers)]
    ring = [(2 * z, 2 * ((z + 1) % chips)) for z in range(chips)]
    ring += [(2 * z + 1, 2 * ((z - 1) % chips) + 1) for z in range(chips)]

    def swap(block):
        return lax.ppermute(block, "seq", partner)

    def turn(block):
        return lax.ppermute(block, "seq", ring)

    digits = jnp.concatenate([cache_pos // POS_BASE, cache_pos % POS_BASE]).astype(jnp.bfloat16)
    digits = digits.reshape(2 * tile // HD, HD)
    digits = jnp.pad(digits, ((0, POS_ROWS - digits.shape[0]), (0, 0)))
    own_keys = jnp.concatenate([cache_keys, digits])[None]
    own_values = cache_values[None]
    own_self = jnp.concatenate([self_keys, self_values], axis=1)[None]
    key_block = jnp.concatenate([own_keys, swap(own_keys)])
    value_block = jnp.concatenate([own_values, swap(own_values)])
    other_self = swap(own_self)
    self_block = jnp.concatenate([own_self, other_self])
    key_groups, value_groups, selfs = [(key_block,)], [(value_block,)], [self_block]
    for step in range(1, chips // 2 + 1):
        key_block = turn(key_block)
        value_block = turn(value_block)
        if step == chips // 2:
            key_groups.append((key_block,))
            value_groups.append((value_block,))
        else:
            key_groups.append((key_block, swap(key_block)))
            value_groups.append((value_block, swap(value_block)))
        if step <= 2:
            self_block = turn(self_block)
            selfs += [self_block, swap(self_block)]

    index = my_index.reshape(1)
    attended, finish, own, back = compute(
        index, query, d_out, key_groups, value_groups, selfs, 3, (rows, tile, start_pos)
    )
    returned = []
    for distance in range(1, rim + 1):
        route = [(i, i - distance) for i in range(distance, peers)]
        returned.append(lax.ppermute(back[rim - distance], "seq", route))
    grad_query = finish()
    grad_keys, grad_values = combine(own, returned)
    return attended, grad_query, grad_keys, grad_values


def solution(mesh):
    split = P(("batch", "seq"), "kvh")
    return jax.shard_map(
        local,
        mesh=mesh,
        in_specs=(split,) * 5 + (P(("batch", "seq")), split),
        out_specs=(split,) * 4,
        check_vma=False,
    )
```

```python
import functools

import jax
import jax.numpy as jnp
from jax import lax
from jax.experimental import pallas as pl
from jax.experimental.pallas import tpu as pltpu
from jax.sharding import PartitionSpec as P


HD = 128
GROUP = 5
WINDOW = 512
LANES = 128
BLOCK = 32
NEG = -1e30
SCALE = HD**-0.5
EXP2_SCALE = SCALE * 1.4426950408889634
POS_BASE = 128
POS_ROWS = 16


def nt(a, b):
    return lax.dot_general(a, b, (((1,), (1,)), ((), ())), preferred_element_type=jnp.float32)


def nn(a, b):
    return lax.dot_general(a, b, (((1,), (0,)), ((), ())), preferred_element_type=jnp.float32)


def tn(a, b):
    return lax.dot_general(a, b, (((0,), (0,)), ((), ())), preferred_element_type=jnp.float32)


def cuts(width, step):
    return [slice(i, i + step) for i in range(0, width, step)]


def positions_of(digits, groups):
    wide = digits.astype(jnp.float32)
    return wide[:groups] * POS_BASE + wide[groups : 2 * groups]


def row_bound(base, rows, start_pos):
    row = lax.broadcasted_iota(jnp.int32, (rows, LANES), 0)
    bound = start_pos + jnp.maximum(base + row - (WINDOW - 1), 0)
    return bound.astype(jnp.float32)


def window_visible(base, rows, window, g):
    row = lax.broadcasted_iota(jnp.int32, (rows, LANES), 0)
    key = lax.broadcasted_iota(jnp.int32, (rows, LANES), 1) + g * LANES
    first = window - rows
    return (key <= row + first) & (key >= row + (first - WINDOW + 1)) & (key >= first - base)


def accumulate(parts, row_max, row_sum, rs):
    old = row_max[rs, :]
    best = old
    for part in parts:
        best = jnp.maximum(best, part)
    added = row_sum[rs, :] * jnp.exp2((old - best) * EXP2_SCALE)
    raised = [jnp.exp2((part - best) * EXP2_SCALE) for part in parts]
    for part in raised:
        added = added + part
    row_max[rs, :] = best
    row_sum[rs, :] = added
    return raised, best


def packet_stats(queries, keys, digits, bound, state, rows, t):
    row_max, row_sum, raised_ref, level_ref = state
    lanes = cuts(keys.shape[0], LANES)
    positions = positions_of(digits, len(lanes))
    scores = nt(queries, keys)
    for rs in cuts(rows * GROUP, BLOCK):
        inner = slice(rs.start % rows, rs.start % rows + BLOCK)
        limit = bound[inner]
        parts = [
            jnp.where(positions[g : g + 1] < limit, scores[rs, ls], NEG)
            for g, ls in enumerate(lanes)
        ]
        raised, best = accumulate(parts, row_max, row_sum, rs)
        for ls, part in zip(lanes, raised):
            raised_ref[t, rs, ls] = part
        level_ref[t, rs, :] = best


def stats_kernel(*refs, rows, tile, start_pos, counts, done, with_window):
    meta_ref = refs[0]
    first_packet = 2 if done else 3
    packets = refs[first_packet : first_packet + len(counts)]
    at = first_packet + len(counts) + (5 if with_window else 0) + (4 if done else 0)
    outs = refs[at:]
    state = outs[:4]
    if done:
        queries_ref = refs[1]
    else:
        queries_ref, grads_ref = outs[4:]
        for h in range(GROUP):
            queries_ref[h * rows : (h + 1) * rows, :] = refs[1][:, h * HD : (h + 1) * HD]
            grads_ref[h * rows : (h + 1) * rows, :] = refs[2][:, h * HD : (h + 1) * HD]
    row_max, row_sum = state[:2]
    base = meta_ref[0] * rows
    bound = row_bound(base, rows, start_pos)
    if done:
        max_in, sum_in = refs[at - 4 : at - 2]
        row_max[...] = max_in[...]
        row_sum[...] = sum_in[...]
    else:
        row_max[...] = jnp.full(row_max.shape, NEG, jnp.float32)
        row_sum[...] = jnp.zeros(row_sum.shape, jnp.float32)
    t = done
    for packet, count in zip(packets, counts):

        def one(n, carry, packet=packet, t=t):
            packet_stats(
                queries_ref[...],
                packet[n, :tile, :],
                packet[n, tile : tile + POS_ROWS, :],
                bound,
                state,
                rows,
                t + n,
            )
            return carry

        lax.fori_loop(0, count, one, 0)
        t += count
    if with_window:
        self_raised, self_level, window_ref = outs[4:]
        own, up_one, swapped_one, up_two, swapped_two = refs[first_packet + len(counts) :][:5]
        even = meta_ref[0] % 2 == 0

        def place(blocks):
            for d, block in enumerate(blocks):
                window_ref[d * rows : (d + 1) * rows, :] = block

        @pl.when(even)
        def _():
            place([up_two[0], up_two[1], up_one[0], up_one[1], own[0]])

        @pl.when(jnp.logical_not(even))
        def _():
            place([swapped_two[1], swapped_one[0], swapped_one[1], own[1], own[0]])

        window = window_ref.shape[0]
        scores = nt(queries_ref[...], window_ref[:, :HD])
        lanes = cuts(window, LANES)
        shown = [window_visible(base, rows, window, g) for g in range(len(lanes))]
        for rs in cuts(rows * GROUP, BLOCK):
            inner = slice(rs.start % rows, rs.start % rows + BLOCK)
            parts = [
                jnp.where(shown[g][inner], scores[rs, ls], NEG) for g, ls in enumerate(lanes)
            ]
            raised, best = accumulate(parts, row_max, row_sum, rs)
            for ls, part in zip(lanes, raised):
                self_raised[rs, ls] = part
            self_level[rs, :] = best


WHOLE = pl.BlockSpec(memory_space=pltpu.VMEM)
ANYWHERE = pl.BlockSpec(memory_space=pl.ANY)
SCALARS = pl.BlockSpec(memory_space=pltpu.SMEM)
LIMIT = pltpu.CompilerParams(vmem_limit_bytes=6 * 1024 * 1024)


def f32(*shape):
    return jax.ShapeDtypeStruct(shape, jnp.float32)


def bf16(*shape):
    return jax.ShapeDtypeStruct(shape, jnp.bfloat16)


def stats(my_index, inputs, previous, packets, selfs, done, tiles, rows, tile, start_pos):
    total = rows * GROUP
    counts = tuple(p.shape[0] for p in packets)
    operands = [my_index, *inputs, *packets]
    outs = [f32(total, LANES), f32(total, LANES), f32(tiles, total, tile), f32(tiles, total, LANES)]
    aliases = {}
    if selfs is not None:
        operands += list(selfs)
        span = (WINDOW // rows + 1) * rows
        outs += [f32(total, span), f32(total, LANES), bf16(span, 2 * HD)]
    if previous is None:
        outs += [bf16(total, HD)] * 2
    else:
        aliases = {len(operands) + 2: 2, len(operands) + 3: 3}
        operands += list(previous)
    keys = sum(counts) * tile
    return pl.pallas_call(
        functools.partial(
            stats_kernel,
            rows=rows,
            tile=tile,
            start_pos=start_pos,
            counts=counts,
            done=done,
            with_window=selfs is not None,
        ),
        in_specs=[SCALARS] + [WHOLE] * (len(operands) - 1),
        out_specs=[WHOLE] * len(outs),
        out_shape=outs,
        input_output_aliases=aliases,
        compiler_params=LIMIT,
        cost_estimate=pl.CostEstimate(
            flops=2 * total * HD * keys, transcendentals=total * keys, bytes_accessed=2 * keys * HD
        ),
        name="stats",
    )(*operands)


def fetch_all(packets, counts, held, sems, width):
    copies = []
    at = 0
    for n, count in enumerate(counts):
        copy = pltpu.make_async_copy(
            packets[n].at[:, pl.ds(0, width), :], held.at[pl.ds(at, count)], sems.at[n]
        )
        copy.start()
        copies.append(copy)
        at += count
    return copies


def value_kernel(*refs, rows, tile, counts):
    n = len(counts)
    meta_ref = refs[0]
    (queries, grads, window_ref, max_in, sum_in, raised, level, self_raised, self_level) = refs[1:10]
    key_packets = refs[10 : 10 + n]
    value_packets = refs[10 + n : 10 + 2 * n]
    outs = refs[10 + 2 * n :]
    (attended_ref, factor_ref, delta, partial_ref, keys, values, own_ref, give_ref, keep_ref) = outs[:9]
    (top_ref, inverse_ref, summed, self_weights, key_sems, value_sems) = outs[9:]
    even = meta_ref[0] % 2 == 0

    def hand_out(grad, cs):
        four, three, two, one, own = (grad[at, :] for at in cuts(window, rows))
        nothing = jnp.zeros_like(own)
        own_ref[:, cs] = own
        give_ref[0, :, cs] = jnp.where(even, three, two).astype(jnp.bfloat16)
        give_ref[1, :, cs] = jnp.where(even, four, three).astype(jnp.bfloat16)
        give_ref[2, :, cs] = jnp.where(even, nothing, one).astype(jnp.bfloat16)
        keep_ref[0, :, cs] = jnp.where(even, one, four)
        keep_ref[1, :, cs] = jnp.where(even, two, nothing)

    copies = fetch_all(value_packets, counts, values, value_sems, tile)
    key_copies = fetch_all(key_packets, counts, keys, key_sems, tile)
    total = rows * GROUP
    window = window_ref.shape[0]
    tiles = sum(counts)
    heads = cuts(total, rows)
    cols = cuts(GROUP * HD, HD)
    lanes = cuts(tile, LANES)
    self_lanes = cuts(window, LANES)
    for hs in heads:
        best = max_in[hs, :]
        top = jnp.max(best, axis=1, keepdims=True)
        scaled = sum_in[hs, :] * jnp.exp2((best - top) * EXP2_SCALE)
        top_ref[hs, :] = jnp.broadcast_to(top, (rows, LANES))
        inverse = 1.0 / jnp.sum(scaled, axis=1, keepdims=True)
        inverse_ref[hs, :] = jnp.broadcast_to(inverse, (rows, LANES))

    parts = []
    for hs in heads:
        factor = jnp.exp2((self_level[hs, :] - top_ref[hs, :]) * EXP2_SCALE) * inverse_ref[hs, :]
        pieces = []
        for ls in self_lanes:
            weight = self_raised[hs, ls] * factor
            self_weights[hs, ls] = weight
            pieces.append(weight.astype(jnp.bfloat16))
        parts.append(jnp.concatenate(pieces, axis=1))
    rounded = jnp.concatenate(parts, axis=0)
    summed[...] = nn(rounded, window_ref[:, HD:])
    hand_out(tn(rounded, grads[...]), slice(HD, 2 * HD))
    for copy in copies:
        copy.wait()

    def value_pass(t, carry):
        parts = []
        for hs in heads:
            factor = jnp.exp2((level[t, hs, :] - top_ref[hs, :]) * EXP2_SCALE) * inverse_ref[hs, :]
            factor_ref[t, hs, :] = factor
            pieces = [(raised[t, hs, ls] * factor).astype(jnp.bfloat16) for ls in lanes]
            parts.append(jnp.concatenate(pieces, axis=1))
        summed[...] += nn(jnp.concatenate(parts, axis=0), values[t])
        return carry

    lax.fori_loop(0, tiles, value_pass, 0)
    for hs, cs in zip(heads, cols):
        out = summed[hs, :].astype(jnp.bfloat16)
        attended_ref[:, cs] = out
        products = out.astype(jnp.float32) * grads[hs, :].astype(jnp.float32)
        delta[hs, :] = jnp.broadcast_to(jnp.sum(products, axis=1, keepdims=True), (rows, LANES))

    grad_weights = nt(grads[...], window_ref[:, HD:])
    parts = []
    for hs in heads:
        shift = delta[hs, :]
        pieces = [
            (self_weights[hs, ls] * (grad_weights[hs, ls] - shift)).astype(jnp.bfloat16)
            for ls in self_lanes
        ]
        parts.append(jnp.concatenate(pieces, axis=1))
    grad_scores = jnp.concatenate(parts, axis=0)
    partial_ref[...] = nn(grad_scores, window_ref[:, :HD])
    hand_out(tn(grad_scores, queries[...]), slice(0, HD))
    for copy in key_copies:
        copy.wait()


def grad_kernel(
    grads, raised, factor_ref, delta, partial_ref, keys, values, out_ref, *scratch, rows, span, last
):
    heads = cuts(rows * GROUP, rows)
    cols = cuts(GROUP * HD, HD)
    lanes = cuts(keys.shape[1], LANES)
    summed = scratch[0] if last else out_ref
    summed[...] = partial_ref[...]

    def grad_pass(t, carry):
        grad_weights = nt(grads[...], values[t])
        parts = []
        for hs in heads:
            shift = delta[hs, :]
            factor = factor_ref[t, hs, :]
            pieces = [
                (raised[t, hs, ls] * factor * (grad_weights[hs, ls] - shift)).astype(jnp.bfloat16)
                for ls in lanes
            ]
            parts.append(jnp.concatenate(pieces, axis=1))
        summed[...] += nn(jnp.concatenate(parts, axis=0), keys[t])
        return carry

    lax.fori_loop(*span, grad_pass, 0)
    if last:
        for hs, cs in zip(heads, cols):
            out_ref[:, cs] = (summed[hs, :] * SCALE).astype(jnp.bfloat16)


def merge_kernel(keep_ref, swapped_ref, out_ref):
    for n in range(2):
        out_ref[n] = (keep_ref[n] + swapped_ref[n].astype(jnp.float32)).astype(jnp.bfloat16)


def combine_kernel(meta_ref, own_ref, swapped_ref, near_ref, far_ref, keys_ref, values_ref):
    mine = 1 - meta_ref[0] % 2
    total = own_ref[...] + swapped_ref[2].astype(jnp.float32)
    total = total + near_ref[mine].astype(jnp.float32) + far_ref[mine].astype(jnp.float32)
    keys_ref[...] = (total[:, :HD] * SCALE).astype(jnp.bfloat16)
    values_ref[...] = total[:, HD:].astype(jnp.bfloat16)


def value_stage(my_index, queries, grads, window, state, key_packets, value_packets, rows, tile):
    counts = tuple(p.shape[0] for p in value_packets)
    tiles = sum(counts)
    total = rows * GROUP
    span = window.shape[0]
    return pl.pallas_call(
        functools.partial(value_kernel, rows=rows, tile=tile, counts=counts),
        in_specs=[SCALARS] + [WHOLE] * 9 + [ANYWHERE] * (2 * len(counts)),
        out_specs=[WHOLE] * 9,
        out_shape=[
            bf16(rows, GROUP * HD),
            f32(tiles, total, LANES),
            f32(total, LANES),
            f32(total, HD),
            bf16(tiles, tile, HD),
            bf16(tiles, tile, HD),
            f32(rows, 2 * HD),
            bf16(3, rows, 2 * HD),
            f32(2, rows, 2 * HD),
        ],
        scratch_shapes=[
            pltpu.VMEM((total, LANES), jnp.float32),
            pltpu.VMEM((total, LANES), jnp.float32),
            pltpu.VMEM((total, HD), jnp.float32),
            pltpu.VMEM((total, span), jnp.float32),
            pltpu.SemaphoreType.DMA((len(counts),)),
            pltpu.SemaphoreType.DMA((len(counts),)),
        ],
        input_output_aliases={7: 1},
        compiler_params=LIMIT,
        cost_estimate=pl.CostEstimate(
            flops=2 * total * HD * tiles * tile, transcendentals=0, bytes_accessed=tiles * tile * HD
        ),
        name="value_stage",
    )(my_index, queries, grads, window, *state, *key_packets, *value_packets)


def grad_stage(grads, raised, factor, delta, partial, keys, values, rows, span, last):
    tiles, tile, _ = keys.shape
    total = rows * GROUP
    return pl.pallas_call(
        functools.partial(grad_kernel, rows=rows, span=span, last=last),
        in_specs=[WHOLE] * 7,
        out_specs=WHOLE,
        out_shape=bf16(rows, GROUP * HD) if last else f32(total, HD),
        scratch_shapes=[pltpu.VMEM((total, HD), jnp.float32)] if last else [],
        compiler_params=LIMIT,
        cost_estimate=pl.CostEstimate(
            flops=4 * total * HD * (span[1] - span[0]) * tile,
            transcendentals=0,
            bytes_accessed=tiles * tile * HD,
        ),
        name="grad_stage",
    )(grads, raised, factor, delta, partial, keys, values)


def merge(keep, swapped):
    return pl.pallas_call(
        merge_kernel,
        in_specs=[WHOLE] * 2,
        out_specs=WHOLE,
        out_shape=bf16(*keep.shape),
        compiler_params=LIMIT,
        name="merge",
    )(keep, swapped)


def combine(my_index, own, swapped, near, far):
    rows = own.shape[0]
    return pl.pallas_call(
        combine_kernel,
        in_specs=[SCALARS] + [WHOLE] * 4,
        out_specs=[WHOLE] * 2,
        out_shape=[bf16(rows, HD)] * 2,
        compiler_params=LIMIT,
        name="combine",
    )(my_index, own, swapped, near, far)


def compute(index, query, d_out, key_groups, value_groups, selfs, selfs_at, shape):
    rows, tile, start_pos = shape
    tiles = sum(p.shape[0] for group in key_groups for p in group)
    state, done = None, 0
    for n, group in enumerate(key_groups):
        inputs = [queries] if done else [query, d_out]
        extra = selfs if n == selfs_at else None
        outs = stats(index, inputs, state, group, extra, done, tiles, rows, tile, start_pos)
        state = outs[:4]
        if not done:
            queries, grads = outs[4:]
        elif extra is not None:
            *self_state, window = outs[4:]
        done += sum(p.shape[0] for p in group)
    key_packets = [p for group in key_groups for p in group]
    value_packets = [p for group in value_groups for p in group]
    attended, factor, delta, partial, keys, values, own, give, keep = value_stage(
        index, queries, grads, window, [*state, *self_state], key_packets, value_packets, rows, tile
    )

    def finish():
        shared = (grads, state[2], factor, delta)
        summed = grad_stage(*shared, partial, keys, values, rows, (0, tiles // 2), False)
        return grad_stage(*shared, summed, keys, values, rows, (tiles // 2, tiles), True)

    return attended, finish, own, give, keep


def local(query, self_keys, self_values, cache_keys, cache_values, cache_pos, d_out):
    rows = query.shape[0]
    tile = cache_keys.shape[0]
    peers = lax.axis_size("seq")
    my_index = lax.axis_index("seq")
    start_pos = (tile - rows) * peers
    chips = peers // 2

    partner = [(i, i ^ 1) for i in range(peers)]
    ring = [(2 * z, 2 * ((z + 1) % chips)) for z in range(chips)]
    ring += [(2 * z + 1, 2 * ((z - 1) % chips) + 1) for z in range(chips)]

    def swap(block):
        return lax.ppermute(block, "seq", partner)

    def turn(block):
        return lax.ppermute(block, "seq", ring)

    digits = jnp.concatenate([cache_pos // POS_BASE, cache_pos % POS_BASE]).astype(jnp.bfloat16)
    digits = digits.reshape(2 * tile // HD, HD)
    digits = jnp.pad(digits, ((0, POS_ROWS - digits.shape[0]), (0, 0)))
    own_keys = jnp.concatenate([cache_keys, digits])[None]
    own_values = cache_values[None]
    own_self = jnp.concatenate([self_keys, self_values], axis=1)[None]
    key_block = jnp.concatenate([own_keys, swap(own_keys)])
    value_block = jnp.concatenate([own_values, swap(own_values)])
    other_self = swap(own_self)
    self_block = jnp.concatenate([own_self, other_self])
    key_groups, value_groups, selfs = [(key_block,)], [(value_block,)], [self_block]
    for step in range(1, chips // 2 + 1):
        key_block = turn(key_block)
        value_block = turn(value_block)
        if step == chips // 2:
            key_groups.append((key_block,))
            value_groups.append((value_block,))
        else:
            key_groups.append((key_block, swap(key_block)))
            value_groups.append((value_block, swap(value_block)))
        if step <= 2:
            self_block = turn(self_block)
            selfs += [self_block, swap(self_block)]

    index = my_index.reshape(1)
    attended, finish, own, give, keep = compute(
        index, query, d_out, key_groups, value_groups, selfs, 3, (rows, tile, start_pos)
    )
    back = [(2 * z, 2 * z - 2) for z in range(1, chips)]
    back += [(2 * z + 1, 2 * z - 3) for z in range(2, chips)]
    swapped = swap(give)
    near = lax.ppermute(merge(keep, swapped), "seq", back)
    far = swap(near)
    grad_query = finish()
    grad_keys, grad_values = combine(index, own, swapped, near, far)
    return attended, grad_query, grad_keys, grad_values


def solution(mesh):
    split = P(("batch", "seq"), "kvh")
    return jax.shard_map(
        local,
        mesh=mesh,
        in_specs=(split,) * 5 + (P(("batch", "seq")), split),
        out_specs=(split,) * 4,
        check_vma=False,
    )
```

```python
import functools

import jax
import jax.numpy as jnp
from jax import lax
from jax.experimental import pallas as pl
from jax.experimental.pallas import tpu as pltpu
from jax.sharding import PartitionSpec as P


HD = 128
GROUP = 5
WINDOW = 512
LANES = 128
BLOCK = 32
NEG = -1e30
SCALE = HD**-0.5
EXP2_SCALE = SCALE * 1.4426950408889634
POS_BASE = 128
POS_ROWS = 16


def nt(a, b):
    return lax.dot_general(a, b, (((1,), (1,)), ((), ())), preferred_element_type=jnp.float32)


def nn(a, b):
    return lax.dot_general(a, b, (((1,), (0,)), ((), ())), preferred_element_type=jnp.float32)


def tn(a, b):
    return lax.dot_general(a, b, (((0,), (0,)), ((), ())), preferred_element_type=jnp.float32)


def cuts(width, step):
    return [slice(i, i + step) for i in range(0, width, step)]


def positions_of(digits, groups):
    wide = digits.astype(jnp.float32)
    return wide[:groups] * POS_BASE + wide[groups : 2 * groups]


def row_bound(base, rows, start_pos):
    row = lax.broadcasted_iota(jnp.int32, (rows, LANES), 0)
    bound = start_pos + jnp.maximum(base + row - (WINDOW - 1), 0)
    return bound.astype(jnp.float32)


def window_visible(base, rows, window, g):
    row = lax.broadcasted_iota(jnp.int32, (rows, LANES), 0)
    key = lax.broadcasted_iota(jnp.int32, (rows, LANES), 1) + g * LANES
    first = window - rows
    return (key <= row + first) & (key >= row + (first - WINDOW + 1)) & (key >= first - base)


def accumulate(parts, row_max, row_sum, rs):
    old = row_max[rs, :]
    best = old
    for part in parts:
        best = jnp.maximum(best, part)
    added = row_sum[rs, :] * jnp.exp2((old - best) * EXP2_SCALE)
    raised = [jnp.exp2((part - best) * EXP2_SCALE) for part in parts]
    for part in raised:
        added = added + part
    row_max[rs, :] = best
    row_sum[rs, :] = added
    return raised, best


def packet_stats(queries, keys, digits, bound, state, rows, t):
    row_max, row_sum, raised_ref, level_ref = state
    lanes = cuts(keys.shape[0], LANES)
    positions = positions_of(digits, len(lanes))
    scores = nt(queries, keys)
    for rs in cuts(rows * GROUP, BLOCK):
        inner = slice(rs.start % rows, rs.start % rows + BLOCK)
        limit = bound[inner]
        parts = [
            jnp.where(positions[g : g + 1] < limit, scores[rs, ls], NEG)
            for g, ls in enumerate(lanes)
        ]
        raised, best = accumulate(parts, row_max, row_sum, rs)
        for ls, part in zip(lanes, raised):
            raised_ref[t, rs, ls] = part
        level_ref[t, rs, :] = best


def stats_kernel(*refs, rows, tile, start_pos, counts, done, with_window):
    meta_ref = refs[0]
    first_packet = 2 if done else 3
    packets = refs[first_packet : first_packet + len(counts)]
    at = first_packet + len(counts) + (5 if with_window else 0) + (4 if done else 0)
    outs = refs[at:]
    state = outs[:4]
    if done:
        queries_ref = refs[1]
    else:
        queries_ref, grads_ref = outs[4:]
        for h in range(GROUP):
            queries_ref[h * rows : (h + 1) * rows, :] = refs[1][:, h * HD : (h + 1) * HD]
            grads_ref[h * rows : (h + 1) * rows, :] = refs[2][:, h * HD : (h + 1) * HD]
    row_max, row_sum = state[:2]
    base = meta_ref[0] * rows
    bound = row_bound(base, rows, start_pos)
    if done:
        max_in, sum_in = refs[at - 4 : at - 2]
        row_max[...] = max_in[...]
        row_sum[...] = sum_in[...]
    else:
        row_max[...] = jnp.full(row_max.shape, NEG, jnp.float32)
        row_sum[...] = jnp.zeros(row_sum.shape, jnp.float32)
    t = done
    for packet, count in zip(packets, counts):

        def one(n, carry, packet=packet, t=t):
            packet_stats(
                queries_ref[...],
                packet[n, :tile, :],
                packet[n, tile : tile + POS_ROWS, :],
                bound,
                state,
                rows,
                t + n,
            )
            return carry

        lax.fori_loop(0, count, one, 0)
        t += count
    if with_window:
        self_raised, self_level, window_ref = outs[4:]
        own, up_one, swapped_one, up_two, swapped_two = refs[first_packet + len(counts) :][:5]
        even = meta_ref[0] % 2 == 0

        def place(blocks):
            for d, block in enumerate(blocks):
                window_ref[d * rows : (d + 1) * rows, :] = block

        @pl.when(even)
        def _():
            place([up_two[0], up_two[1], up_one[0], up_one[1], own[0]])

        @pl.when(jnp.logical_not(even))
        def _():
            place([swapped_two[1], swapped_one[0], swapped_one[1], own[1], own[0]])

        window = window_ref.shape[0]
        scores = nt(queries_ref[...], window_ref[:, :HD])
        lanes = cuts(window, LANES)
        shown = [window_visible(base, rows, window, g) for g in range(len(lanes))]
        for rs in cuts(rows * GROUP, BLOCK):
            inner = slice(rs.start % rows, rs.start % rows + BLOCK)
            parts = [
                jnp.where(shown[g][inner], scores[rs, ls], NEG) for g, ls in enumerate(lanes)
            ]
            raised, best = accumulate(parts, row_max, row_sum, rs)
            for ls, part in zip(lanes, raised):
                self_raised[rs, ls] = part
            self_level[rs, :] = best


WHOLE = pl.BlockSpec(memory_space=pltpu.VMEM)
ANYWHERE = pl.BlockSpec(memory_space=pl.ANY)
SCALARS = pl.BlockSpec(memory_space=pltpu.SMEM)
LIMIT = pltpu.CompilerParams(vmem_limit_bytes=6 * 1024 * 1024)


def f32(*shape):
    return jax.ShapeDtypeStruct(shape, jnp.float32)


def bf16(*shape):
    return jax.ShapeDtypeStruct(shape, jnp.bfloat16)


def stats(my_index, inputs, previous, packets, selfs, done, tiles, rows, tile, start_pos):
    total = rows * GROUP
    counts = tuple(p.shape[0] for p in packets)
    operands = [my_index, *inputs, *packets]
    outs = [f32(total, LANES), f32(total, LANES), f32(tiles, total, tile), f32(tiles, total, LANES)]
    aliases = {}
    if selfs is not None:
        operands += list(selfs)
        span = (WINDOW // rows + 1) * rows
        outs += [f32(total, span), f32(total, LANES), bf16(span, 2 * HD)]
    if previous is None:
        outs += [bf16(total, HD)] * 2
    else:
        aliases = {len(operands) + 2: 2, len(operands) + 3: 3}
        operands += list(previous)
    keys = sum(counts) * tile
    return pl.pallas_call(
        functools.partial(
            stats_kernel,
            rows=rows,
            tile=tile,
            start_pos=start_pos,
            counts=counts,
            done=done,
            with_window=selfs is not None,
        ),
        in_specs=[SCALARS] + [WHOLE] * (len(operands) - 1),
        out_specs=[WHOLE] * len(outs),
        out_shape=outs,
        input_output_aliases=aliases,
        compiler_params=LIMIT,
        cost_estimate=pl.CostEstimate(
            flops=2 * total * HD * keys, transcendentals=total * keys, bytes_accessed=2 * keys * HD
        ),
        name="stats",
    )(*operands)


def fetch_all(packets, counts, held, sems, width):
    copies = []
    at = 0
    for n, count in enumerate(counts):
        copy = pltpu.make_async_copy(
            packets[n].at[:, pl.ds(0, width), :], held.at[pl.ds(at, count)], sems.at[n]
        )
        copy.start()
        copies.append(copy)
        at += count
    return copies


def value_kernel(*refs, rows, tile, counts):
    n = len(counts)
    meta_ref = refs[0]
    (queries, grads, window_ref, max_in, sum_in, raised, level, self_raised, self_level) = refs[1:10]
    key_packets = refs[10 : 10 + n]
    value_packets = refs[10 + n : 10 + 2 * n]
    outs = refs[10 + 2 * n :]
    (attended_ref, factor_ref, delta, partial_ref, keys, values, own_ref, give_ref, keep_ref) = outs[:9]
    (top_ref, inverse_ref, summed, self_weights, key_sems, value_sems) = outs[9:]
    even = meta_ref[0] % 2 == 0

    def hand_out(grad, cs):
        four, three, two, one, own = (grad[at, :] for at in cuts(window, rows))
        nothing = jnp.zeros_like(own)
        own_ref[:, cs] = own
        give_ref[0, :, cs] = jnp.where(even, three, two).astype(jnp.bfloat16)
        give_ref[1, :, cs] = jnp.where(even, four, three).astype(jnp.bfloat16)
        give_ref[2, :, cs] = jnp.where(even, nothing, one).astype(jnp.bfloat16)
        keep_ref[0, :, cs] = jnp.where(even, one, four)
        keep_ref[1, :, cs] = jnp.where(even, two, nothing)

    copies = fetch_all(value_packets, counts, values, value_sems, tile)
    key_copies = fetch_all(key_packets, counts, keys, key_sems, tile)
    total = rows * GROUP
    window = window_ref.shape[0]
    tiles = sum(counts)
    heads = cuts(total, rows)
    cols = cuts(GROUP * HD, HD)
    lanes = cuts(tile, LANES)
    self_lanes = cuts(window, LANES)
    for hs in heads:
        best = max_in[hs, :]
        top = jnp.max(best, axis=1, keepdims=True)
        scaled = sum_in[hs, :] * jnp.exp2((best - top) * EXP2_SCALE)
        top_ref[hs, :] = jnp.broadcast_to(top, (rows, LANES))
        inverse = 1.0 / jnp.sum(scaled, axis=1, keepdims=True)
        inverse_ref[hs, :] = jnp.broadcast_to(inverse, (rows, LANES))

    parts = []
    for hs in heads:
        factor = jnp.exp2((self_level[hs, :] - top_ref[hs, :]) * EXP2_SCALE) * inverse_ref[hs, :]
        pieces = []
        for ls in self_lanes:
            weight = self_raised[hs, ls] * factor
            self_weights[hs, ls] = weight
            pieces.append(weight.astype(jnp.bfloat16))
        parts.append(jnp.concatenate(pieces, axis=1))
    rounded = jnp.concatenate(parts, axis=0)
    summed[...] = nn(rounded, window_ref[:, HD:])
    hand_out(tn(rounded, grads[...]), slice(HD, 2 * HD))
    for copy in copies:
        copy.wait()

    def value_pass(t, carry):
        parts = []
        for hs in heads:
            factor = jnp.exp2((level[t, hs, :] - top_ref[hs, :]) * EXP2_SCALE) * inverse_ref[hs, :]
            factor_ref[t, hs, :] = factor
            pieces = [(raised[t, hs, ls] * factor).astype(jnp.bfloat16) for ls in lanes]
            parts.append(jnp.concatenate(pieces, axis=1))
        summed[...] += nn(jnp.concatenate(parts, axis=0), values[t])
        return carry

    lax.fori_loop(0, tiles, value_pass, 0)
    for hs, cs in zip(heads, cols):
        out = summed[hs, :].astype(jnp.bfloat16)
        attended_ref[:, cs] = out
        products = out.astype(jnp.float32) * grads[hs, :].astype(jnp.float32)
        delta[hs, :] = jnp.broadcast_to(jnp.sum(products, axis=1, keepdims=True), (rows, LANES))

    grad_weights = nt(grads[...], window_ref[:, HD:])
    parts = []
    for hs in heads:
        shift = delta[hs, :]
        pieces = [
            (self_weights[hs, ls] * (grad_weights[hs, ls] - shift)).astype(jnp.bfloat16)
            for ls in self_lanes
        ]
        parts.append(jnp.concatenate(pieces, axis=1))
    grad_scores = jnp.concatenate(parts, axis=0)
    partial_ref[...] = nn(grad_scores, window_ref[:, :HD])
    hand_out(tn(grad_scores, queries[...]), slice(0, HD))
    for copy in key_copies:
        copy.wait()


def grad_kernel(
    grads, raised, factor_ref, delta, partial_ref, keys, values, out_ref, *scratch, rows, span, last
):
    heads = cuts(rows * GROUP, rows)
    cols = cuts(GROUP * HD, HD)
    lanes = cuts(keys.shape[1], LANES)
    summed = scratch[0] if last else out_ref
    summed[...] = partial_ref[...]

    def grad_pass(t, carry):
        grad_weights = nt(grads[...], values[t])
        parts = []
        for hs in heads:
            shift = delta[hs, :]
            factor = factor_ref[t, hs, :]
            pieces = [
                (raised[t, hs, ls] * factor * (grad_weights[hs, ls] - shift)).astype(jnp.bfloat16)
                for ls in lanes
            ]
            parts.append(jnp.concatenate(pieces, axis=1))
        summed[...] += nn(jnp.concatenate(parts, axis=0), keys[t])
        return carry

    lax.fori_loop(*span, grad_pass, 0)
    if last:
        for hs, cs in zip(heads, cols):
            out_ref[:, cs] = (summed[hs, :] * SCALE).astype(jnp.bfloat16)


def merge_kernel(keep_ref, swapped_ref, out_ref):
    for n in range(2):
        out_ref[n] = (keep_ref[n] + swapped_ref[n].astype(jnp.float32)).astype(jnp.bfloat16)


def combine_kernel(meta_ref, own_ref, swapped_ref, near_ref, far_ref, keys_ref, values_ref):
    mine = 1 - meta_ref[0] % 2
    total = own_ref[...] + swapped_ref[2].astype(jnp.float32)
    total = total + near_ref[mine].astype(jnp.float32) + far_ref[mine].astype(jnp.float32)
    keys_ref[...] = (total[:, :HD] * SCALE).astype(jnp.bfloat16)
    values_ref[...] = total[:, HD:].astype(jnp.bfloat16)


def value_stage(my_index, queries, grads, window, state, key_packets, value_packets, rows, tile):
    counts = tuple(p.shape[0] for p in value_packets)
    tiles = sum(counts)
    total = rows * GROUP
    span = window.shape[0]
    return pl.pallas_call(
        functools.partial(value_kernel, rows=rows, tile=tile, counts=counts),
        in_specs=[SCALARS] + [WHOLE] * 9 + [ANYWHERE] * (2 * len(counts)),
        out_specs=[WHOLE] * 9,
        out_shape=[
            bf16(rows, GROUP * HD),
            f32(tiles, total, LANES),
            f32(total, LANES),
            f32(total, HD),
            bf16(tiles, tile, HD),
            bf16(tiles, tile, HD),
            f32(rows, 2 * HD),
            bf16(3, rows, 2 * HD),
            f32(2, rows, 2 * HD),
        ],
        scratch_shapes=[
            pltpu.VMEM((total, LANES), jnp.float32),
            pltpu.VMEM((total, LANES), jnp.float32),
            pltpu.VMEM((total, HD), jnp.float32),
            pltpu.VMEM((total, span), jnp.float32),
            pltpu.SemaphoreType.DMA((len(counts),)),
            pltpu.SemaphoreType.DMA((len(counts),)),
        ],
        input_output_aliases={7: 1},
        compiler_params=LIMIT,
        cost_estimate=pl.CostEstimate(
            flops=2 * total * HD * tiles * tile, transcendentals=0, bytes_accessed=tiles * tile * HD
        ),
        name="value_stage",
    )(my_index, queries, grads, window, *state, *key_packets, *value_packets)


def grad_stage(grads, raised, factor, delta, partial, keys, values, rows, span, last):
    tiles, tile, _ = keys.shape
    total = rows * GROUP
    return pl.pallas_call(
        functools.partial(grad_kernel, rows=rows, span=span, last=last),
        in_specs=[WHOLE] * 7,
        out_specs=WHOLE,
        out_shape=bf16(rows, GROUP * HD) if last else f32(total, HD),
        scratch_shapes=[pltpu.VMEM((total, HD), jnp.float32)] if last else [],
        compiler_params=LIMIT,
        cost_estimate=pl.CostEstimate(
            flops=4 * total * HD * (span[1] - span[0]) * tile,
            transcendentals=0,
            bytes_accessed=tiles * tile * HD,
        ),
        name="grad_stage",
    )(grads, raised, factor, delta, partial, keys, values)


def merge(keep, swapped):
    return pl.pallas_call(
        merge_kernel,
        in_specs=[WHOLE] * 2,
        out_specs=WHOLE,
        out_shape=bf16(*keep.shape),
        compiler_params=LIMIT,
        name="merge",
    )(keep, swapped)


def combine(my_index, own, swapped, near, far):
    rows = own.shape[0]
    return pl.pallas_call(
        combine_kernel,
        in_specs=[SCALARS] + [WHOLE] * 4,
        out_specs=[WHOLE] * 2,
        out_shape=[bf16(rows, HD)] * 2,
        compiler_params=LIMIT,
        name="combine",
    )(my_index, own, swapped, near, far)


def compute(index, query, d_out, key_groups, value_groups, selfs, selfs_at, shape):
    rows, tile, start_pos = shape
    tiles = sum(p.shape[0] for group in key_groups for p in group)
    state, done = None, 0
    for n, group in enumerate(key_groups):
        inputs = [queries] if done else [query, d_out]
        extra = selfs if n == selfs_at else None
        outs = stats(index, inputs, state, group, extra, done, tiles, rows, tile, start_pos)
        state = outs[:4]
        if not done:
            queries, grads = outs[4:]
        elif extra is not None:
            *self_state, window = outs[4:]
        done += sum(p.shape[0] for p in group)
    key_packets = [p for group in key_groups for p in group]
    value_packets = [p for group in value_groups for p in group]
    attended, factor, delta, partial, keys, values, own, give, keep = value_stage(
        index, queries, grads, window, [*state, *self_state], key_packets, value_packets, rows, tile
    )

    def finish():
        shared = (grads, state[2], factor, delta)
        one, two = tiles // 4, tiles - tiles // 4
        summed = grad_stage(*shared, partial, keys, values, rows, (0, one), False)
        summed = grad_stage(*shared, summed, keys, values, rows, (one, two), False)
        return grad_stage(*shared, summed, keys, values, rows, (two, tiles), True)

    return attended, finish, own, give, keep


def local(query, self_keys, self_values, cache_keys, cache_values, cache_pos, d_out):
    rows = query.shape[0]
    tile = cache_keys.shape[0]
    peers = lax.axis_size("seq")
    my_index = lax.axis_index("seq")
    start_pos = (tile - rows) * peers
    chips = peers // 2

    partner = [(i, i ^ 1) for i in range(peers)]
    ring = [(2 * z, 2 * ((z + 1) % chips)) for z in range(chips)]
    ring += [(2 * z + 1, 2 * ((z - 1) % chips) + 1) for z in range(chips)]

    def swap(block):
        return lax.ppermute(block, "seq", partner)

    def turn(block):
        return lax.ppermute(block, "seq", ring)

    digits = jnp.concatenate([cache_pos // POS_BASE, cache_pos % POS_BASE]).astype(jnp.bfloat16)
    digits = digits.reshape(2 * tile // HD, HD)
    digits = jnp.pad(digits, ((0, POS_ROWS - digits.shape[0]), (0, 0)))
    own_keys = jnp.concatenate([cache_keys, digits])[None]
    own_values = cache_values[None]
    own_self = jnp.concatenate([self_keys, self_values], axis=1)[None]
    key_block = jnp.concatenate([own_keys, swap(own_keys)])
    value_block = jnp.concatenate([own_values, swap(own_values)])
    other_self = swap(own_self)
    self_block = jnp.concatenate([own_self, other_self])
    key_groups, value_groups, selfs = [(key_block,)], [(value_block,)], [self_block]
    for step in range(1, chips // 2 + 1):
        key_block = turn(key_block)
        value_block = turn(value_block)
        if step == chips // 2:
            key_groups.append((key_block,))
            value_groups.append((value_block,))
        else:
            key_groups.append((key_block, swap(key_block)))
            value_groups.append((value_block, swap(value_block)))
        if step <= 2:
            self_block = turn(self_block)
            selfs += [self_block, swap(self_block)]

    index = my_index.reshape(1)
    attended, finish, own, give, keep = compute(
        index, query, d_out, key_groups, value_groups, selfs, 3, (rows, tile, start_pos)
    )
    back = [(2 * z, 2 * z - 2) for z in range(1, chips)]
    back += [(2 * z + 1, 2 * z - 3) for z in range(2, chips)]
    swapped = swap(give)
    near = lax.ppermute(merge(keep, swapped), "seq", back)
    far = swap(near)
    grad_query = finish()
    grad_keys, grad_values = combine(index, own, swapped, near, far)
    return attended, grad_query, grad_keys, grad_values


def solution(mesh):
    split = P(("batch", "seq"), "kvh")
    return jax.shard_map(
        local,
        mesh=mesh,
        in_specs=(split,) * 5 + (P(("batch", "seq")), split),
        out_specs=(split,) * 4,
        check_vma=False,
    )
```
